32 devices in a mesh: ep: 8 (over y, x, core), tp: 4 (over z).
Axes of the slice: x: 2, y: 2, z: 4, core: 2. Of those that a mesh axis runs over, the one named last changes fastest.
Arguments:
- block_input: bfloat16 [2048, 2880], P('ep'), may hold values from -6 to 6
- segment_ids: int32 [2048], P('ep'), may hold values from 0 to 47, never falling along the last dimension, each value on 1 to 128 neighbouring positions
- expert_ids: int32 [2048, 4], P('ep'), may hold values from 0 to 7, all different within a row; in each aligned block of 256 rows (0 to 255, 256 to 511, ...) at most 192 rows name the same one
- expert_gates: float32 [2048, 4], P('ep'), may hold values from 0.05 to 0.6
- attn_norm_gain: bfloat16 [2880], P('ep'), may hold values from 0.5 to 1.5
- query_weight: bfloat16 [2880, 4096], P('ep', 'tp'), may hold values from -8 to 8
- key_weight: bfloat16 [2880, 512], P('ep', 'tp'), may hold values from -1 to 1
- value_projection: bfloat16 [2880, 512], P('ep', 'tp'), may hold values from -0.109375 to 0.109375
- query_bias: bfloat16 [64, 64], P('tp', 'ep'), may hold values from -3 to 3
- key_head_bias: bfloat16 [8, 64], P('tp', 'ep'), may hold values from -3 to 3
- value_head_bias: bfloat16 [8, 64], P('tp', 'ep'), may hold values from -3 to 3
- sink_head_logits: bfloat16 [64], P('tp'), may hold values from 0 to 4
- output_weight: bfloat16 [4096, 2880], P('tp', 'ep'), may hold values from -0.375 to 0.375
- output_bias: bfloat16 [2880], P('ep'), may hold values from -3 to 3
- ffn_norm_gain: bfloat16 [2880], P('ep'), may hold values from 0.5 to 1.5
- gate_weight: bfloat16 [8, 2880, 2880], P('ep', None, 'tp'), may hold values from -0.109375 to 0.109375
- up_weight: bfloat16 [8, 2880, 2880], P('ep', None, 'tp'), may hold values from -0.109375 to 0.109375
- gate_bias: bfloat16 [8, 2880], P('ep', 'tp'), may hold values from -8 to 8
- up_bias: bfloat16 [8, 2880], P('ep', 'tp'), may hold values from -8 to 8
- down_weight: bfloat16 [8, 2880, 2880], P('ep', 'tp'), may hold values from -0.109375 to 0.109375
- down_bias: bfloat16 [8, 2880], P('ep'), may hold values from -3 to 3
- cotangent: bfloat16 [2048, 2880], P('ep'), may hold values from -6 to 6
Outputs:
- block_result: bfloat16 [2048, 2880], P('ep', 'tp')
- block_input_grad: bfloat16 [2048, 2880], P('ep')
- attention_gain_grad: float32 [2880], P('ep')
- query_projection_grad: float32 [2880, 4096], P('ep', 'tp')
- key_projection_grad: float32 [2880, 512], P('ep', 'tp')
- value_projection_grad: float32 [2880, 512], P('ep', 'tp')
- query_bias_grad: float32 [64, 64], P('tp', 'ep')
- key_bias_grad: float32 [8, 64], P('tp', 'ep')
- value_bias_grad: float32 [8, 64], P('tp', 'ep')
- sink_logit_grad: float32 [64], P('tp')
- output_projection_grad: float32 [4096, 2880], P('tp', 'ep')
- output_offset_grad: float32 [2880], P('ep')
- feedforward_gain_grad: float32 [2880], P('ep')
- gate_weight_grad: float32 [8, 2880, 2880], P('ep', None, 'tp')
- up_weight_grad: float32 [8, 2880, 2880], P('ep', None, 'tp')
- gate_bias_grad: float32 [8, 2880], P('ep', 'tp')
- up_bias_grad: float32 [8, 2880], P('ep', 'tp')
- down_weight_grad: float32 [8, 2880, 2880], P('ep', 'tp')
- down_bias_grad: float32 [8, 2880], P('ep')
The draws below stay inside these ranges and needn't reach their ends.
Inputs may be any that keep to these rules, and one draw needn't show every extreme that they name: `segment_ids`: segment numbers never fall along the tokens; a segment spans 1 to 128 positions, one exactly that many. `expert_ids`: each token names 4 different experts; among the 256 tokens of one index of ep no expert is named more than 192 times, a bound that some block reaches.
All inputs are finite; a program needn't handle non-finite values.
Results may differ from the reference program's by a relative error of at most 0.018.
Values may be sent and summed in bfloat16 or wider, within the bound.
No kernel may reach another device: no remote copies, remote signals or barrier semaphores. Data moves between devices by JAX's collectives and lax.ppermute only.
A program may use at most 320 MiB of HBM per device.

```python
import math
import jax
import jax.numpy as jnp
import numpy as np
from jax import lax

MODEL_WIDTH = 2880
QUERY_HEADS = 64
KEY_VALUE_HEADS = 8
HEAD_SIZE = 64
FF = 2880
TOP = 4
TOKENS_PER_PART = 256
EXPERTS = 8
TOKEN_TOTAL = 2048
CAP = 192
SEGS = 48
N_EP = 8


def key_projected(key):
    return jax.random.normal(jax.random.fold_in(key, 7001), (MODEL_WIDTH, KEY_VALUE_HEADS * HEAD_SIZE), jnp.float32) * MODEL_WIDTH ** (-0.5)


def draw_key_weight(key, part):
    return jnp.clip(key_projected(key), -1.0, 1.0).astype(jnp.bfloat16)


def draw_query_weight(key, part):
    own = jax.random.normal(jax.random.fold_in(key, 7002), (MODEL_WIDTH, QUERY_HEADS * HEAD_SIZE), jnp.float32) * MODEL_WIDTH ** (-0.5)
    return jnp.clip(own, -8.0, 8.0).astype(jnp.bfloat16)


def steps_of(rng, dims, cuts, low, top_value):
    loudness = 1.0
    for axis_at, blocks in cuts:
        heights = jax.random.uniform(jax.random.fold_in(jax.random.fold_in(rng, 6), axis_at), (blocks,), jnp.float32, low / len(cuts), top_value / len(cuts))
        loudness = loudness * jnp.repeat(jnp.exp(heights), dims[axis_at] // blocks).reshape((-1,) + (1,) * (len(dims) - 1 - axis_at))
    return loudness


def split_up(amount, total, bound, slope):
    weights = [(1 << 20) // math.isqrt(grade ** slope) + 1 for grade in range(2, amount + 1)]
    surplus, counts = total - bound - (amount - 1), [1] * (amount - 1)
    while surplus > 0:
        free = [i for i in range(amount - 1) if counts[i] < bound]
        whole, budget = sum([weights[i] for i in free]), surplus
        for i in free:
            extra = min(bound - counts[i], max(1, budget * weights[i] // whole), surplus)
            counts[i] = counts[i] + extra
            surplus = surplus - extra
    return np.array([bound] + counts)


def uneven_parts(key, number_of, total, most, lean):
    if number_of == 2:
        one = jax.random.randint(key, (), max(1, total - most), min(most, total - 1) + 1)
        return jnp.stack([one, total - one])
    tallies = jnp.asarray(split_up(number_of, total, most, lean), jnp.int32)
    twos = (number_of - 1) // 2
    donor, sink = tallies[1:1 + 2 * twos:2], tallies[2:2 + 2 * twos:2]
    slack = jnp.minimum(donor - 1, most - sink)
    shifted = jax.random.randint(jax.random.fold_in(key, 1), (twos,), 0, 1 << 20) % (slack + 1)
    tallies = tallies.at[1:1 + 2 * twos:2].set(donor - shifted).at[2:2 + 2 * twos:2].set(sink + shifted)
    return tallies[jax.random.permutation(jax.random.fold_in(key, 2), number_of)]


def routed_block(stream_key, own, number, rows, amount, top, bound, slope):
    sequence = jax.random.permutation(stream_key, amount)
    heavy_load, ordinary = load_shares(amount, rows * top, bound, slope, True), load_shares(amount, rows * top, bound, slope, False)
    places = jnp.arange(amount)

    def named(tallies, turn):
        used = int((tallies > 0).sum())
        fixed = max(1, used // 4)
        passed = fixed + (places - fixed + turn * (used - fixed)) % max(1, amount - fixed)
        return jnp.zeros((amount,), jnp.int32).at[sequence[jnp.where(places < fixed, places, passed)]].set(jnp.asarray(tallies, jnp.int32))

    tallies = jnp.where(number % 4 == 0, named(heavy_load, number // 4), named(ordinary, number - number // 4 - 1))
    mixed = jax.random.permutation(jax.random.fold_in(own, 3), amount)
    giver, receiver = mixed[0:amount // 2 * 2:2], mixed[1:amount // 2 * 2:2]
    slack = jnp.minimum(tallies[giver] - 1, bound - tallies[receiver]) // 2
    slack = jnp.where((giver == sequence[0]) | (receiver == sequence[0]) | (tallies[receiver] == 0), 0, jnp.maximum(slack, 0))
    passed = jax.random.randint(jax.random.fold_in(own, 4), (amount // 2,), 0, 1 << 20) % (slack + 1)
    tallies = tallies.at[giver].add(-passed).at[receiver].add(passed)
    items = jnp.searchsorted(jnp.cumsum(tallies), jnp.arange(rows * top), side="right").astype(jnp.int32)
    listing = items.reshape(top, rows).T
    listing = listing[jax.random.permutation(jax.random.fold_in(own, 1), rows)]
    turn = jax.random.randint(jax.random.fold_in(own, 2), (rows, 1), 0, top)
    return jnp.take_along_axis(listing, (jnp.arange(top)[None, :] + turn) % top, axis=1)


def load_shares(count, total, limit, slope, full):
    portions = [(1 << 20) // math.isqrt(rank ** slope) + 1 for rank in range(1, count + 1)]
    largest = limit if full else min(limit, max(-(-total // count), total * portions[0] // sum(portions)))
    least = 1 if total - largest >= count - 1 else 0
    given, spare = [largest] + [least] * (count - 1), total - largest - least * (count - 1)
    while spare > 0:
        free = [i for i in range(1, count) if given[i] < largest] or [i for i in range(1, count) if given[i] < limit]
        mass, budget = sum([portions[i] for i in free]), spare
        for i in free:
            addition = min(limit - given[i], max(1, budget * portions[i] // mass), spare)
            given[i] = given[i] + addition
            spare = spare - addition
    return np.array(given)


def scatter_about(stream_key, shape, scale, most, cuts=(), kind=jnp.bfloat16):
    result = jax.random.normal(stream_key, shape, jnp.float32) * scale
    if len(cuts) > 0:
        result = steps_of(stream_key, shape, cuts, -0.22, 0.18) * result
    return jnp.clip(result, min=-most, max=most).astype(kind)


def setup_inputs(seed: int = 0) -> dict:
    arg_keys = jax.random.split(jax.random.key(seed), 23)
    block_input = scatter_about(arg_keys[0], (TOKEN_TOTAL, MODEL_WIDTH), 1.0, 6.0, ((0, 8),))
    segment_ids = jnp.searchsorted(jnp.cumsum(uneven_parts(arg_keys[1], SEGS, TOKEN_TOTAL, TOKENS_PER_PART // 2, 2)), jnp.arange(TOKEN_TOTAL), side="right").astype(jnp.int32)
    expert_ids_keys = jax.random.split(jax.random.fold_in(arg_keys[2], 1), TOKEN_TOTAL // TOKENS_PER_PART)
    expert_ids_turns = jax.random.permutation(jax.random.fold_in(arg_keys[2], 3), TOKEN_TOTAL // TOKENS_PER_PART)
    expert_ids = jax.vmap(lambda own, number: routed_block(jax.random.fold_in(arg_keys[2], 2), own, number, TOKENS_PER_PART, EXPERTS, TOP, CAP, 1))(expert_ids_keys, expert_ids_turns).reshape((TOKEN_TOTAL, TOP))
    expert_gates = jnp.clip(0.05 + 0.55 * jax.random.uniform(arg_keys[3], (TOKEN_TOTAL, TOP), jnp.float32) ** steps_of(arg_keys[3], (TOKEN_TOTAL, TOP), ((0, 8),), -0.2, 0.2), 0.05, 0.6)
    attn_norm_gain = jnp.clip(1.0 + 0.1 * jax.random.normal(arg_keys[4], (MODEL_WIDTH,), jnp.float32), 0.5, 1.5).astype(jnp.bfloat16)
    query_weight = draw_query_weight(jax.random.fold_in(arg_keys[22], 71), 0)
    key_weight = draw_key_weight(jax.random.fold_in(arg_keys[22], 71), 0)
    value_projection = scatter_about(arg_keys[7], (MODEL_WIDTH, KEY_VALUE_HEADS * HEAD_SIZE), MODEL_WIDTH ** -0.5, 0.109375, ((0, 8), (1, 4)))
    query_bias = scatter_about(arg_keys[8], (QUERY_HEADS, HEAD_SIZE), 0.5, 3.0, ((0, 4), (1, 8)))
    key_head_bias = scatter_about(arg_keys[9], (KEY_VALUE_HEADS, HEAD_SIZE), 0.5, 3.0, ((0, 4), (1, 8)))
    value_head_bias = scatter_about(arg_keys[10], (KEY_VALUE_HEADS, HEAD_SIZE), 0.5, 3.0, ((0, 4), (1, 8)))
    sink_head_logits = jnp.clip(4.0 * jax.random.uniform(arg_keys[11], (QUERY_HEADS,), jnp.float32) ** steps_of(arg_keys[11], (QUERY_HEADS,), ((0, 4),), -0.2, 0.2), 0.0, 4.0).astype(jnp.bfloat16)
    output_weight = scatter_about(arg_keys[12], (QUERY_HEADS * HEAD_SIZE, MODEL_WIDTH), (QUERY_HEADS * HEAD_SIZE // 16) ** -0.5, 0.375, ((0, 4), (1, 8)))
    output_bias = scatter_about(arg_keys[13], (MODEL_WIDTH,), 0.5, 3.0, ((0, 8),))
    ffn_norm_gain = jnp.clip(1.0 + 0.1 * jax.random.normal(arg_keys[14], (MODEL_WIDTH,), jnp.float32), 0.5, 1.5).astype(jnp.bfloat16)
    gate_weight = scatter_about(arg_keys[15], (EXPERTS, MODEL_WIDTH, FF), MODEL_WIDTH ** -0.5, 0.109375, ((0, 8), (2, 4)))
    up_weight = scatter_about(arg_keys[16], (EXPERTS, MODEL_WIDTH, FF), MODEL_WIDTH ** -0.5, 0.109375, ((0, 8), (2, 4)))
    gate_bias = scatter_about(arg_keys[17], (EXPERTS, FF), 1.5, 8.0, ((0, 8), (1, 4)))
    up_bias = scatter_about(arg_keys[18], (EXPERTS, FF), 1.5, 8.0, ((0, 8), (1, 4)))
    down_weight = scatter_about(arg_keys[19], (EXPERTS, FF, MODEL_WIDTH), FF ** -0.5, 0.109375, ((0, 8), (1, 4)))
    down_bias = scatter_about(arg_keys[20], (EXPERTS, MODEL_WIDTH), 0.5, 3.0, ((0, 8),))
    cotangent = scatter_about(arg_keys[21], (TOKEN_TOTAL, MODEL_WIDTH), 1.0, 6.0, ((0, 8),))
    return dict(block_input=block_input, segment_ids=segment_ids, expert_ids=expert_ids, expert_gates=expert_gates, attn_norm_gain=attn_norm_gain, query_weight=query_weight, key_weight=key_weight, value_projection=value_projection, query_bias=query_bias, key_head_bias=key_head_bias, value_head_bias=value_head_bias, sink_head_logits=sink_head_logits, output_weight=output_weight, output_bias=output_bias, ffn_norm_gain=ffn_norm_gain, gate_weight=gate_weight, up_weight=up_weight, gate_bias=gate_bias, up_bias=up_bias, down_weight=down_weight, down_bias=down_bias, cotangent=cotangent)


EPSILON = 1e-05
THETA = 150000.0
ALPHA = 1.702
LIMIT = 7.0

def rms_stats(activation):
    inverse = lax.rsqrt(lax.optimization_barrier(jnp.mean(activation * activation, axis=1, keepdims=True)) + EPSILON)
    return (activation * inverse, inverse)

def norm_back(grad_normed, normed, inverse):
    return inverse * (grad_normed - normed * lax.optimization_barrier(jnp.mean(grad_normed * normed, axis=1, keepdims=True)))

def rope_tables(segment_row):
    length = segment_row.shape[0]
    row_index = lax.broadcasted_iota(jnp.int32, (length, length), 0)
    column_index = lax.broadcasted_iota(jnp.int32, (length, length), 1)
    allowed = (segment_row[:, None] == segment_row[None, :]) & (column_index <= row_index)
    position = lax.optimization_barrier(jnp.sum(allowed.astype(jnp.float32), axis=1)) - 1.0
    frequency = THETA ** (-2.0 * jnp.arange(HEAD_SIZE // 2, dtype=jnp.float32) / HEAD_SIZE)
    angles = position[:, None] * frequency[None, :]
    return (allowed, jnp.cos(angles), jnp.sin(angles))

def rotate(heads, cosine_table, sine_table):
    half_dim = HEAD_SIZE // 2
    first_half = heads[..., :half_dim]
    second_half = heads[..., half_dim:]
    cosine = cosine_table[:, None, :]
    sine_rows = sine_table[:, None, :]
    return jnp.concatenate([first_half * cosine - second_half * sine_rows, second_half * cosine + first_half * sine_rows], axis=-1)

def unrotate(gradient_set, cosine_table, sine_table):
    half_dim = HEAD_SIZE // 2
    first_half = gradient_set[..., :half_dim]
    second_half = gradient_set[..., half_dim:]
    cosine = cosine_table[:, None, :]
    sine_rows = sine_table[:, None, :]
    return jnp.concatenate([first_half * cosine + second_half * sine_rows, second_half * cosine - first_half * sine_rows], axis=-1)

def attention_scores(grouped_query, keys_rot, allowed):
    scores = jnp.einsum('qgha,kga->ghqk', grouped_query.astype(jnp.float32), keys_rot.astype(jnp.float32)) * HEAD_SIZE ** (-0.5)
    return jnp.where(allowed[None, None], scores, -jnp.inf)

def expert_hidden(rows, gate_matrix, up_matrix, gate_shift, up_shift):
    gate_pre = jnp.dot(rows, gate_matrix, preferred_element_type=jnp.float32) + gate_shift.astype(jnp.float32)
    up_pre = jnp.dot(rows, up_matrix, preferred_element_type=jnp.float32) + up_shift.astype(jnp.float32)
    gate_clip = jnp.minimum(gate_pre, LIMIT)
    up_clip = jnp.clip(up_pre, -LIMIT, LIMIT)
    sigmoid_gate = jax.nn.sigmoid(ALPHA * gate_clip)
    glu_part = gate_clip * sigmoid_gate
    hidden = ((up_clip + 1.0) * glu_part).astype(jnp.bfloat16)
    return (gate_pre, up_pre, gate_clip, up_clip, sigmoid_gate, glu_part, hidden)

def reference(block_input, segment_ids, expert_ids, expert_gates, attn_norm_gain, query_weight, key_weight, value_projection, query_bias, key_head_bias, value_head_bias, sink_head_logits, output_weight, output_bias, ffn_norm_gain, gate_weight, up_weight, gate_bias, up_bias, down_weight, down_bias, cotangent):
    query_group_width = QUERY_HEADS // KEY_VALUE_HEADS
    scale_factor = HEAD_SIZE ** (-0.5)
    sink_logit_grid = sink_head_logits.astype(jnp.float32).reshape(KEY_VALUE_HEADS, query_group_width)[:, :, None]
    inputs = block_input.astype(jnp.float32)
    attn_normed, attn_inverse = rms_stats(inputs)
    attn_scale = attn_norm_gain.astype(jnp.float32)
    attn_in = (attn_normed * attn_scale).astype(jnp.bfloat16)
    query_heads = jnp.dot(attn_in, query_weight, preferred_element_type=jnp.float32) + query_bias.astype(jnp.float32).reshape(-1)
    key_heads = jnp.dot(attn_in, key_weight, preferred_element_type=jnp.float32) + key_head_bias.astype(jnp.float32).reshape(-1)
    value_heads = jnp.dot(attn_in, value_projection, preferred_element_type=jnp.float32) + value_head_bias.astype(jnp.float32).reshape(-1)
    segment_block_mask = segment_ids.reshape(N_EP, TOKENS_PER_PART)

    def forward_pass(pieces):
        segment_row, query_rows, key_rows, value_rows = pieces
        allowed, cosine_table, sine_table = rope_tables(segment_row)
        rotated_query = rotate(query_rows, cosine_table, sine_table).astype(jnp.bfloat16)
        keys_rot = rotate(key_rows, cosine_table, sine_table).astype(jnp.bfloat16)
        value_cast = value_rows.astype(jnp.bfloat16)
        grouped_heads = rotated_query.reshape(TOKENS_PER_PART, KEY_VALUE_HEADS, query_group_width, HEAD_SIZE)
        scores = attention_scores(grouped_heads, keys_rot, allowed)
        top_score = jnp.maximum(lax.optimization_barrier(jnp.max(scores, axis=3)), sink_logit_grid)
        total = lax.optimization_barrier(jnp.sum(jnp.exp(scores - top_score[..., None]), axis=3)) + jnp.exp(sink_logit_grid - top_score)
        log_total = top_score + jnp.log(total)
        probability = jnp.exp(scores - log_total[..., None]).astype(jnp.bfloat16)
        attended_rows = jnp.einsum('ghqk,kga->qgha', probability.astype(jnp.float32), value_cast.astype(jnp.float32))
        attended_rows = attended_rows.reshape(TOKENS_PER_PART, QUERY_HEADS * HEAD_SIZE).astype(jnp.bfloat16)
        return (rotated_query, keys_rot, value_cast, log_total, attended_rows)
    kept_entries = lax.map(forward_pass, (segment_block_mask, query_heads.reshape(N_EP, TOKENS_PER_PART, QUERY_HEADS, HEAD_SIZE), key_heads.reshape(N_EP, TOKENS_PER_PART, KEY_VALUE_HEADS, HEAD_SIZE), value_heads.reshape(N_EP, TOKENS_PER_PART, KEY_VALUE_HEADS, HEAD_SIZE)))
    attended_all = kept_entries[4].reshape(TOKEN_TOTAL, QUERY_HEADS * HEAD_SIZE)
    residual = inputs + (jnp.dot(attended_all, output_weight, preferred_element_type=jnp.float32) + output_bias.astype(jnp.float32))
    ffn_normed, ffn_inverse = rms_stats(residual)
    ffn_scale = ffn_norm_gain.astype(jnp.float32)
    ffn_in = (ffn_normed * ffn_scale).astype(jnp.bfloat16)
    flat_ids = expert_ids.reshape(-1)
    flat_gates = expert_gates.reshape(-1)
    route_count = N_EP * CAP
    expert_list = jnp.arange(EXPERTS, dtype=jnp.int32)

    def expert_rows(expert):
        matches = flat_ids == expert
        chosen = jnp.nonzero(matches, size=route_count, fill_value=0)[0].astype(jnp.int32)
        valid = jnp.arange(route_count, dtype=jnp.int32) < jnp.sum(matches.astype(jnp.int32))
        return (chosen, valid)

    def moe_step(total, pieces):
        expert, gate_matrix, up_matrix, gate_shift, up_shift, down_matrix, down_shift = pieces
        chosen, valid = expert_rows(expert)
        token_rows = chosen // TOP
        parts = expert_hidden(ffn_in[token_rows], gate_matrix, up_matrix, gate_shift, up_shift)
        output_rows = (jnp.dot(parts[6], down_matrix, preferred_element_type=jnp.float32) + down_shift.astype(jnp.float32)).astype(jnp.bfloat16)
        weights = jnp.where(valid, flat_gates[chosen], 0.0)
        return (total.at[token_rows].add(weights[:, None] * output_rows.astype(jnp.float32)), None)
    moe = lax.scan(moe_step, jnp.zeros((TOKEN_TOTAL, MODEL_WIDTH), jnp.float32), (expert_list, gate_weight, up_weight, gate_bias, up_bias, down_weight, down_bias))[0]
    block_result = (residual + moe).astype(jnp.bfloat16)
    grad_out = cotangent.astype(jnp.float32)

    def moe_back(total, pieces):
        expert, gate_matrix, up_matrix, gate_shift, up_shift, down_matrix, down_shift = pieces
        chosen, valid = expert_rows(expert)
        token_rows = chosen // TOP
        rows = ffn_in[token_rows]
        gate_pre, up_pre, gate_clip, up_clip, sigmoid_gate, glu_part, hidden = expert_hidden(rows, gate_matrix, up_matrix, gate_shift, up_shift)
        weights = jnp.where(valid, flat_gates[chosen], 0.0)
        row_grads = (weights[:, None] * grad_out[token_rows]).astype(jnp.bfloat16)
        hidden_grad = jnp.dot(row_grads, down_matrix.T, preferred_element_type=jnp.float32)
        down_grad = jnp.dot(hidden.T, row_grads, preferred_element_type=jnp.float32)
        down_shift_grad = lax.optimization_barrier(jnp.sum(row_grads.astype(jnp.float32), axis=0))
        up_grad = jnp.where((up_pre > -LIMIT) & (up_pre < LIMIT), hidden_grad * glu_part, 0.0)
        gate_grad = jnp.where(gate_pre < LIMIT, hidden_grad * (up_clip + 1.0) * (sigmoid_gate + ALPHA * gate_clip * sigmoid_gate * (1.0 - sigmoid_gate)), 0.0)
        gate_cast = gate_grad.astype(jnp.bfloat16)
        up_cast = up_grad.astype(jnp.bfloat16)
        gate_matrix_grad = jnp.dot(rows.T, gate_cast, preferred_element_type=jnp.float32)
        up_matrix_grad = jnp.dot(rows.T, up_cast, preferred_element_type=jnp.float32)
        input_rows = (jnp.dot(gate_cast, gate_matrix.T, preferred_element_type=jnp.float32) + jnp.dot(up_cast, up_matrix.T, preferred_element_type=jnp.float32)).astype(jnp.bfloat16)
        total = total.at[token_rows].add(jnp.where(valid[:, None], input_rows.astype(jnp.float32), 0.0))
        return (total, (gate_matrix_grad, up_matrix_grad, lax.optimization_barrier(jnp.sum(gate_grad, axis=0)), lax.optimization_barrier(jnp.sum(up_grad, axis=0)), down_grad, down_shift_grad))
    ffn_in_grad, expert_gradients = lax.scan(moe_back, jnp.zeros((TOKEN_TOTAL, MODEL_WIDTH), jnp.float32), (expert_list, gate_weight, up_weight, gate_bias, up_bias, down_weight, down_bias))
    feedforward_gain_grad = lax.optimization_barrier(jnp.sum(ffn_in_grad * ffn_normed, axis=0))
    residual_grad = grad_out + norm_back(ffn_in_grad * ffn_scale, ffn_normed, ffn_inverse)
    output_offset_grad = lax.optimization_barrier(jnp.sum(residual_grad, axis=0))
    residual_cast = residual_grad.astype(jnp.bfloat16)
    output_projection_grad = jnp.dot(attended_all.T, residual_cast, preferred_element_type=jnp.float32)
    attended_grad = jnp.dot(residual_cast, output_weight.T, preferred_element_type=jnp.float32).astype(jnp.bfloat16)

    def backward_sequence(pieces):
        segment_row, rotated_query, keys_rot, value_cast, log_total, attended_rows, row_gradients = pieces
        allowed, cosine_table, sine_table = rope_tables(segment_row)
        grouped_heads = rotated_query.reshape(TOKENS_PER_PART, KEY_VALUE_HEADS, query_group_width, HEAD_SIZE)
        head_gradients = row_gradients.reshape(TOKENS_PER_PART, KEY_VALUE_HEADS, query_group_width, HEAD_SIZE).astype(jnp.float32)
        softmax_delta = jnp.einsum('nxiz,nxiz->xin', head_gradients, attended_rows.reshape(TOKENS_PER_PART, KEY_VALUE_HEADS, query_group_width, HEAD_SIZE).astype(jnp.float32))
        scores = attention_scores(grouped_heads, keys_rot, allowed)
        probability = jnp.exp(scores - log_total[..., None])
        prob_cast = probability.astype(jnp.bfloat16).astype(jnp.float32)
        value_gradient = jnp.einsum('ghqk,qgha->kga', prob_cast, head_gradients)
        prob_grad = jnp.einsum('qgha,kga->ghqk', head_gradients, value_cast.astype(jnp.float32))
        score_grad = (probability * (prob_grad - softmax_delta[..., None])).astype(jnp.bfloat16).astype(jnp.float32)
        query_gradient = jnp.einsum('ghqk,kga->qgha', score_grad, keys_rot.astype(jnp.float32)) * scale_factor
        key_gradient = jnp.einsum('ghqk,qgha->kga', score_grad, grouped_heads.astype(jnp.float32)) * scale_factor
        sink_weight_term = -lax.optimization_barrier(jnp.sum(jnp.exp(sink_logit_grid - log_total) * softmax_delta, axis=2))
        query_gradient = unrotate(query_gradient.reshape(TOKENS_PER_PART, QUERY_HEADS, HEAD_SIZE), cosine_table, sine_table)
        key_gradient = unrotate(key_gradient, cosine_table, sine_table)
        return (query_gradient.reshape(TOKENS_PER_PART, QUERY_HEADS * HEAD_SIZE), key_gradient.reshape(TOKENS_PER_PART, KEY_VALUE_HEADS * HEAD_SIZE), value_gradient.reshape(TOKENS_PER_PART, KEY_VALUE_HEADS * HEAD_SIZE), sink_weight_term)
    gradient_set = lax.map(backward_sequence, (segment_block_mask, kept_entries[0], kept_entries[1], kept_entries[2], kept_entries[3], kept_entries[4], attended_grad.reshape(N_EP, TOKENS_PER_PART, QUERY_HEADS * HEAD_SIZE)))
    query_gradient = gradient_set[0].reshape(TOKEN_TOTAL, QUERY_HEADS * HEAD_SIZE)
    key_gradient = gradient_set[1].reshape(TOKEN_TOTAL, KEY_VALUE_HEADS * HEAD_SIZE)
    value_gradient = gradient_set[2].reshape(TOKEN_TOTAL, KEY_VALUE_HEADS * HEAD_SIZE)
    sink_logit_grad = lax.optimization_barrier(jnp.sum(gradient_set[3], axis=0)).reshape(QUERY_HEADS)
    query_cast = query_gradient.astype(jnp.bfloat16)
    key_cast = key_gradient.astype(jnp.bfloat16)
    value_cast_grad = value_gradient.astype(jnp.bfloat16)
    query_projection_grad = jnp.dot(attn_in.T, query_cast, preferred_element_type=jnp.float32)
    key_projection_grad = jnp.dot(attn_in.T, key_cast, preferred_element_type=jnp.float32)
    value_projection_grad = jnp.dot(attn_in.T, value_cast_grad, preferred_element_type=jnp.float32)
    attn_in_grad = jnp.dot(query_cast, query_weight.T, preferred_element_type=jnp.float32) + jnp.dot(key_cast, key_weight.T, preferred_element_type=jnp.float32) + jnp.dot(value_cast_grad, value_projection.T, preferred_element_type=jnp.float32)
    attention_gain_grad = lax.optimization_barrier(jnp.sum(attn_in_grad * attn_normed, axis=0))
    block_input_grad = (residual_grad + norm_back(attn_in_grad * attn_scale, attn_normed, attn_inverse)).astype(jnp.bfloat16)
    return (block_result, block_input_grad, attention_gain_grad, query_projection_grad, key_projection_grad, value_projection_grad, lax.optimization_barrier(jnp.sum(query_gradient, axis=0)).reshape(QUERY_HEADS, HEAD_SIZE), lax.optimization_barrier(jnp.sum(key_gradient, axis=0)).reshape(KEY_VALUE_HEADS, HEAD_SIZE), lax.optimization_barrier(jnp.sum(value_gradient, axis=0)).reshape(KEY_VALUE_HEADS, HEAD_SIZE), sink_logit_grad, output_projection_grad, output_offset_grad, feedforward_gain_grad, expert_gradients[0], expert_gradients[1], expert_gradients[2], expert_gradients[3], expert_gradients[4], expert_gradients[5])
```

```python
import jax
import jax.numpy as jnp
from jax import lax
from jax.sharding import PartitionSpec as P

QUERY_HEADS = 64
KEY_VALUE_HEADS = 8
HEAD_SIZE = 64
TOP = 4


EPSILON = 1e-05
THETA = 150000.0
ALPHA = 1.702
LIMIT = 7.0


def rms_stats(activation):
    inverse = lax.rsqrt(jnp.mean(activation * activation, axis=1, keepdims=True) + EPSILON)
    return (activation * inverse, inverse)


def norm_back(grad_normed, normed, inverse):
    return inverse * (grad_normed - normed * jnp.mean(grad_normed * normed, axis=1, keepdims=True))


def rope_tables(segment_row):
    length = segment_row.shape[0]
    row_index = lax.broadcasted_iota(jnp.int32, (length, length), 0)
    column_index = lax.broadcasted_iota(jnp.int32, (length, length), 1)
    allowed = (segment_row[:, None] == segment_row[None, :]) & (column_index <= row_index)
    position = jnp.sum(allowed.astype(jnp.float32), axis=1) - 1.0
    frequency = THETA ** (-2.0 * jnp.arange(HEAD_SIZE // 2, dtype=jnp.float32) / HEAD_SIZE)
    angles = position[:, None] * frequency[None, :]
    return (allowed, jnp.cos(angles), jnp.sin(angles))


def rotate(heads, cosine_table, sine_table):
    half_dim = HEAD_SIZE // 2
    first_half = heads[..., :half_dim]
    second_half = heads[..., half_dim:]
    cosine = cosine_table[:, None, :]
    sine_rows = sine_table[:, None, :]
    return jnp.concatenate(
        [
            first_half * cosine - second_half * sine_rows,
            second_half * cosine + first_half * sine_rows,
        ],
        axis=-1,
    )


def unrotate(gradient_set, cosine_table, sine_table):
    half_dim = HEAD_SIZE // 2
    first_half = gradient_set[..., :half_dim]
    second_half = gradient_set[..., half_dim:]
    cosine = cosine_table[:, None, :]
    sine_rows = sine_table[:, None, :]
    return jnp.concatenate(
        [
            first_half * cosine + second_half * sine_rows,
            second_half * cosine - first_half * sine_rows,
        ],
        axis=-1,
    )


def attention_scores(grouped_query, keys_rot, allowed):
    scores = jnp.einsum(
        "qgha,kga->ghqk", grouped_query, keys_rot, preferred_element_type=jnp.float32
    ) * HEAD_SIZE ** (-0.5)
    return jnp.where(allowed[None, None], scores, -jnp.inf)


def shards_routed(
    block_input,
    segment_ids,
    expert_ids,
    expert_gates,
    attn_norm_gain,
    query_weight,
    key_weight,
    value_projection,
    query_bias,
    key_head_bias,
    value_head_bias,
    sink_head_logits,
    output_weight,
    output_bias,
    ffn_norm_gain,
    gate_weight,
    up_weight,
    gate_bias,
    up_bias,
    down_weight,
    down_bias,
    cotangent,
):
    ep_count = lax.axis_size("ep")
    tp_index = lax.axis_index("tp")
    token_count = block_input.shape[0]
    width = block_input.shape[1]
    quarter = width // lax.axis_size("tp")
    local_experts = gate_weight.shape[0]
    experts_all = local_experts * ep_count
    capacity = 3 * token_count * TOP // (2 * experts_all)
    query_group_width = QUERY_HEADS // KEY_VALUE_HEADS
    scale_factor = HEAD_SIZE ** (-0.5)
    (
        attn_scale,
        ffn_scale,
        query_matrix,
        key_matrix,
        value_matrix,
        query_shift,
        key_shift,
        value_shift,
        out_matrix,
        out_shift,
    ) = (
        lax.all_gather(attn_norm_gain, "ep", axis=0, tiled=True),
        lax.all_gather(ffn_norm_gain, "ep", axis=0, tiled=True),
        lax.all_gather(query_weight, "ep", axis=0, tiled=True),
        lax.all_gather(key_weight, "ep", axis=0, tiled=True),
        lax.all_gather(value_projection, "ep", axis=0, tiled=True),
        lax.all_gather(query_bias, "ep", axis=1, tiled=True),
        lax.all_gather(key_head_bias, "ep", axis=1, tiled=True),
        lax.all_gather(value_head_bias, "ep", axis=1, tiled=True),
        lax.all_gather(output_weight, "ep", axis=1, tiled=True),
        lax.all_gather(output_bias, "ep", axis=0, tiled=True),
    )
    attn_scale = attn_scale.astype(jnp.float32)
    ffn_scale = ffn_scale.astype(jnp.float32)
    local_heads = query_matrix.shape[1] // HEAD_SIZE
    local_groups = key_matrix.shape[1] // HEAD_SIZE
    sink_logit_grid = sink_head_logits.astype(jnp.float32).reshape(local_groups, query_group_width)[
        :, :, None
    ]
    inputs = block_input.astype(jnp.float32)
    attn_normed, attn_inverse = rms_stats(inputs)
    attn_in = (attn_normed * attn_scale).astype(jnp.bfloat16)
    query_heads = jnp.dot(
        attn_in, query_matrix, preferred_element_type=jnp.float32
    ) + query_shift.astype(jnp.float32).reshape(-1)
    key_heads = jnp.dot(attn_in, key_matrix, preferred_element_type=jnp.float32) + key_shift.astype(
        jnp.float32
    ).reshape(-1)
    value_heads = jnp.dot(
        attn_in, value_matrix, preferred_element_type=jnp.float32
    ) + value_shift.astype(jnp.float32).reshape(-1)
    allowed, cosine_table, sine_table = rope_tables(segment_ids)
    rotated_query = rotate(
        query_heads.reshape(token_count, local_heads, HEAD_SIZE), cosine_table, sine_table
    ).astype(jnp.bfloat16)
    grouped_heads = rotated_query.reshape(token_count, local_groups, query_group_width, HEAD_SIZE)
    keys_rot = rotate(
        key_heads.reshape(token_count, local_groups, HEAD_SIZE), cosine_table, sine_table
    ).astype(jnp.bfloat16)
    value_cast = value_heads.reshape(token_count, local_groups, HEAD_SIZE).astype(jnp.bfloat16)
    scores = attention_scores(grouped_heads, keys_rot, allowed)
    top_score = jnp.maximum(jnp.max(scores, axis=3), sink_logit_grid)
    total = jnp.sum(jnp.exp(scores - top_score[..., None]), axis=3) + jnp.exp(
        sink_logit_grid - top_score
    )
    log_total = top_score + jnp.log(total)
    probability = jnp.exp(scores - log_total[..., None]).astype(jnp.bfloat16)
    attended_rows = jnp.einsum(
        "ghqk,kga->qgha", probability, value_cast, preferred_element_type=jnp.float32
    )
    attended_rows = attended_rows.reshape(token_count, local_heads * HEAD_SIZE).astype(jnp.bfloat16)
    head_part = jnp.dot(attended_rows, out_matrix, preferred_element_type=jnp.float32)
    residual = inputs + (lax.psum(head_part, "tp") + out_shift.astype(jnp.float32))
    ffn_normed, ffn_inverse = rms_stats(residual)
    ffn_in = (ffn_normed * ffn_scale).astype(jnp.bfloat16)
    flat_ids = expert_ids.reshape(-1)
    one_hot = (flat_ids[:, None] == jnp.arange(experts_all, dtype=jnp.int32)[None, :]).astype(
        jnp.int32
    )
    rank_in_expert = jnp.sum((jnp.cumsum(one_hot, axis=0) - one_hot) * one_hot, axis=1)
    slot_index = flat_ids * capacity + rank_in_expert
    source_index = jnp.arange(token_count * TOP, dtype=jnp.int32) // TOP

    def packed(route_values):
        columns = route_values.shape[1]
        holder = (
            jnp.zeros((experts_all * capacity, columns), route_values.dtype)
            .at[slot_index]
            .set(route_values)
        )
        return holder.reshape(ep_count, local_experts * capacity, columns)

    arrived = lax.all_to_all(
        packed(ffn_in[source_index]), "ep", split_axis=0, concat_axis=0, tiled=True
    )
    arrived = arrived.reshape(ep_count, local_experts, capacity, width)
    gate_pre = (
        jnp.einsum("secd,edf->secf", arrived, gate_weight, preferred_element_type=jnp.float32)
        + gate_bias.astype(jnp.float32)[None, :, None, :]
    )
    up_pre = (
        jnp.einsum("secd,edf->secf", arrived, up_weight, preferred_element_type=jnp.float32)
        + up_bias.astype(jnp.float32)[None, :, None, :]
    )
    gate_clip = jnp.minimum(gate_pre, LIMIT)
    up_clip = jnp.clip(up_pre, -LIMIT, LIMIT)
    sigmoid_gate = jax.nn.sigmoid(ALPHA * gate_clip)
    glu_part = gate_clip * sigmoid_gate
    hidden_cast = ((up_clip + 1.0) * glu_part).astype(jnp.bfloat16)
    down_part = jnp.einsum(
        "secf,efd->secd", hidden_cast, down_weight, preferred_element_type=jnp.float32
    )
    down_shift = down_bias.astype(jnp.float32)
    summed = (
        lax.psum(down_part.astype(jnp.bfloat16), "tp").astype(jnp.float32)
        + down_shift[None, :, None, :]
    )
    returned = lax.all_to_all(
        summed.astype(jnp.bfloat16).reshape(ep_count, local_experts * capacity, width),
        "ep",
        split_axis=0,
        concat_axis=0,
        tiled=True,
    )
    results = lax.dynamic_slice_in_dim(
        returned.reshape(experts_all * capacity, width), tp_index * quarter, quarter, 1
    )
    picked = results[slot_index].astype(jnp.float32).reshape(token_count, TOP, quarter)
    moe_share = jnp.sum(picked * expert_gates[:, :, None], axis=1)
    residual_share = lax.dynamic_slice_in_dim(residual, tp_index * quarter, quarter, 1)
    block_result = (residual_share + moe_share).astype(jnp.bfloat16)
    grad_out = cotangent.astype(jnp.float32)
    flat_gates = expert_gates.reshape(-1)[:, None]
    route_grads = (flat_gates * grad_out[source_index]).astype(jnp.bfloat16)
    grad_arrived = lax.all_to_all(
        packed(route_grads), "ep", split_axis=0, concat_axis=0, tiled=True
    )
    grad_arrived = grad_arrived.reshape(ep_count, local_experts, capacity, width)
    hidden_grad = jnp.einsum(
        "secd,efd->secf", grad_arrived, down_weight, preferred_element_type=jnp.float32
    )
    down_weight_grad = jnp.einsum(
        "secf,secd->efd", hidden_cast, grad_arrived, preferred_element_type=jnp.float32
    )
    down_bias_grad = jnp.sum(grad_arrived, axis=(0, 2), dtype=jnp.float32)
    up_grad = jnp.where((up_pre > -LIMIT) & (up_pre < LIMIT), hidden_grad * glu_part, 0.0)
    gate_grad = jnp.where(
        gate_pre < LIMIT,
        hidden_grad
        * (up_clip + 1.0)
        * (sigmoid_gate + ALPHA * gate_clip * sigmoid_gate * (1.0 - sigmoid_gate)),
        0.0,
    )
    gate_bias_grad = jnp.sum(gate_grad, axis=(0, 2))
    up_bias_grad = jnp.sum(up_grad, axis=(0, 2))
    gate_cast = gate_grad.astype(jnp.bfloat16)
    up_cast = up_grad.astype(jnp.bfloat16)
    gate_weight_grad = jnp.einsum(
        "secd,secf->edf", arrived, gate_cast, preferred_element_type=jnp.float32
    )
    up_weight_grad = jnp.einsum(
        "secd,secf->edf", arrived, up_cast, preferred_element_type=jnp.float32
    )
    input_part = jnp.einsum(
        "secf,edf->secd", gate_cast, gate_weight, preferred_element_type=jnp.float32
    ) + jnp.einsum("secf,edf->secd", up_cast, up_weight, preferred_element_type=jnp.float32)
    input_share = lax.psum_scatter(input_part, "tp", scatter_dimension=3, tiled=True).astype(
        jnp.bfloat16
    )
    input_back = lax.all_to_all(
        input_share.reshape(ep_count, local_experts * capacity, quarter),
        "ep",
        split_axis=0,
        concat_axis=0,
        tiled=True,
    )
    route_input = input_back.reshape(experts_all * capacity, quarter)[slot_index].astype(
        jnp.float32
    )
    ffn_grad_share = jnp.sum(route_input.reshape(token_count, TOP, quarter), axis=1)
    ffn_in_grad = lax.all_gather(ffn_grad_share, "tp", axis=1, tiled=True)
    feedforward_gain_grad = jnp.sum(ffn_in_grad * ffn_normed, axis=0)
    residual_grad = grad_out + norm_back(ffn_in_grad * ffn_scale, ffn_normed, ffn_inverse)
    output_offset_grad = jnp.sum(residual_grad, axis=0)
    residual_cast = residual_grad.astype(jnp.bfloat16)
    output_projection_grad = jnp.dot(
        attended_rows.T, residual_cast, preferred_element_type=jnp.float32
    )
    attended_grad = jnp.dot(residual_cast, out_matrix.T, preferred_element_type=jnp.float32).astype(
        jnp.bfloat16
    )
    head_gradients = attended_grad.reshape(token_count, local_groups, query_group_width, HEAD_SIZE)
    softmax_delta = jnp.einsum(
        "nxiz,nxiz->xin",
        head_gradients,
        attended_rows.reshape(token_count, local_groups, query_group_width, HEAD_SIZE),
        preferred_element_type=jnp.float32,
    )
    scores = attention_scores(grouped_heads, keys_rot, allowed)
    probability = jnp.exp(scores - log_total[..., None])
    prob_cast = probability.astype(jnp.bfloat16)
    value_gradient = jnp.einsum(
        "ghqk,qgha->kga", prob_cast, head_gradients, preferred_element_type=jnp.float32
    )
    prob_grad = jnp.einsum(
        "qgha,kga->ghqk", head_gradients, value_cast, preferred_element_type=jnp.float32
    )
    score_grad = (probability * (prob_grad - softmax_delta[..., None])).astype(jnp.bfloat16)
    query_rot_grad = (
        jnp.einsum("ghqk,kga->qgha", score_grad, keys_rot, preferred_element_type=jnp.float32)
        * scale_factor
    )
    keys_rot_grad = (
        jnp.einsum("ghqk,qgha->kga", score_grad, grouped_heads, preferred_element_type=jnp.float32)
        * scale_factor
    )
    sink_weight_term = -jnp.sum(
        jnp.exp(sink_logit_grid - log_total) * softmax_delta, axis=2
    ).reshape(local_heads)
    query_gradient = unrotate(
        query_rot_grad.reshape(token_count, local_heads, HEAD_SIZE), cosine_table, sine_table
    ).reshape(token_count, local_heads * HEAD_SIZE)
    key_gradient = unrotate(keys_rot_grad, cosine_table, sine_table).reshape(
        token_count, local_groups * HEAD_SIZE
    )
    value_gradient = value_gradient.reshape(token_count, local_groups * HEAD_SIZE)
    query_cast = query_gradient.astype(jnp.bfloat16)
    key_cast = key_gradient.astype(jnp.bfloat16)
    value_grad_cast = value_gradient.astype(jnp.bfloat16)
    query_matrix_grad = jnp.dot(attn_in.T, query_cast, preferred_element_type=jnp.float32)
    key_matrix_grad = jnp.dot(attn_in.T, key_cast, preferred_element_type=jnp.float32)
    value_matrix_grad = jnp.dot(attn_in.T, value_grad_cast, preferred_element_type=jnp.float32)
    attn_in_part = (
        jnp.dot(query_cast, query_matrix.T, preferred_element_type=jnp.float32)
        + jnp.dot(key_cast, key_matrix.T, preferred_element_type=jnp.float32)
        + jnp.dot(value_grad_cast, value_matrix.T, preferred_element_type=jnp.float32)
    )
    attn_in_grad = lax.psum(attn_in_part.astype(jnp.bfloat16), "tp").astype(jnp.float32)
    attn_gain_grad = jnp.sum(attn_in_grad * attn_normed, axis=0)
    block_input_grad = (
        residual_grad + norm_back(attn_in_grad * attn_scale, attn_normed, attn_inverse)
    ).astype(jnp.bfloat16)
    sink_rows = jnp.broadcast_to(sink_weight_term[None, :], (ep_count, local_heads))
    summed_grads = (
        lax.psum_scatter(attn_gain_grad, "ep", scatter_dimension=0, tiled=True),
        lax.psum_scatter(feedforward_gain_grad, "ep", scatter_dimension=0, tiled=True),
        lax.psum_scatter(query_matrix_grad, "ep", scatter_dimension=0, tiled=True),
        lax.psum_scatter(key_matrix_grad, "ep", scatter_dimension=0, tiled=True),
        lax.psum_scatter(value_matrix_grad, "ep", scatter_dimension=0, tiled=True),
        lax.psum_scatter(
            jnp.sum(query_gradient, axis=0).reshape(local_heads, HEAD_SIZE),
            "ep",
            scatter_dimension=1,
            tiled=True,
        ),
        lax.psum_scatter(
            jnp.sum(key_gradient, axis=0).reshape(local_groups, HEAD_SIZE),
            "ep",
            scatter_dimension=1,
            tiled=True,
        ),
        lax.psum_scatter(
            jnp.sum(value_gradient, axis=0).reshape(local_groups, HEAD_SIZE),
            "ep",
            scatter_dimension=1,
            tiled=True,
        ),
        lax.psum_scatter(output_projection_grad, "ep", scatter_dimension=1, tiled=True),
        lax.psum_scatter(output_offset_grad, "ep", scatter_dimension=0, tiled=True),
        lax.psum_scatter(sink_rows, "ep", scatter_dimension=0, tiled=True),
    )
    return (
        block_result,
        block_input_grad,
        summed_grads[0],
        summed_grads[2],
        summed_grads[3],
        summed_grads[4],
        summed_grads[5],
        summed_grads[6],
        summed_grads[7],
        summed_grads[10].reshape(local_heads),
        summed_grads[8],
        summed_grads[9],
        summed_grads[1],
        gate_weight_grad,
        up_weight_grad,
        gate_bias_grad,
        up_bias_grad,
        down_weight_grad,
        down_bias_grad,
    )


CORE, ACROSS_X, ACROSS_Y = 1, 2, 4


def hop(value, mask):
    return lax.ppermute(value, "ep", [(i, i ^ mask) for i in range(lax.axis_size("ep"))])


def hop_tp(value, mask):
    return lax.ppermute(value, "tp", [(i, i ^ mask) for i in range(lax.axis_size("tp"))])


def after(value, *others):
    return lax.optimization_barrier((value,) + others)[0]


def halves_of(rows):
    first = (rows // 2 + 7) // 8 * 8
    return first


def gather_plane(own):
    cut = halves_of(own.shape[0])
    from_x = hop(own, ACROSS_X)
    from_y = hop(own, ACROSS_Y)
    diag_first = hop(from_x[:cut], ACROSS_Y)
    diag_last = hop(from_y[cut:], ACROSS_X)
    mine = [[own], [from_x], [from_y], [diag_first, diag_last]]
    pieces = []
    for group in mine:
        pieces.append(group)
        pieces.append([hop(part, CORE) for part in group])
    return pieces


def scatter_plane(part):
    def paired(target):
        theirs = hop(part(target | CORE).astype(jnp.bfloat16), CORE)
        return part(target).astype(jnp.float32) + theirs.astype(jnp.float32)

    diag = paired(6).astype(jnp.bfloat16)
    cut = halves_of(diag.shape[0])
    for_y = hop(diag[:cut], ACROSS_X).astype(jnp.float32)
    for_x = hop(diag[cut:], ACROSS_Y).astype(jnp.float32)
    along_x = paired(2)
    along_y = paired(4)
    along_x = jnp.concatenate([along_x[:cut], along_x[cut:] + for_x], axis=0).astype(jnp.bfloat16)
    along_y = jnp.concatenate([along_y[:cut] + for_y, along_y[cut:]], axis=0).astype(jnp.bfloat16)
    got_x = hop(along_x, ACROSS_X)
    got_y = hop(along_y, ACROSS_Y)
    return paired(0) + got_x.astype(jnp.float32) + got_y.astype(jnp.float32)


def natural_rows(pieces, ep_index):
    rows, columns = pieces[0][0].shape
    holder = jnp.zeros((len(pieces), rows, columns), pieces[0][0].dtype)
    for relative, group in enumerate(pieces):
        at = 0
        for part in group:
            holder = lax.dynamic_update_slice(holder, part[None], (ep_index ^ relative, at, 0))
            at += part.shape[0]
    return holder.reshape(len(pieces) * rows, columns)


def sum_tp_blocks(full, block):
    count = lax.axis_size("tp")
    total = full[:block]
    for relative in range(1, count):
        sent = full[relative * block : (relative + 1) * block].astype(jnp.bfloat16)
        total = total + hop_tp(sent, relative).astype(jnp.float32)
    return total


def gather_tp_blocks(own):
    return [own] + [hop_tp(own, relative) for relative in range(1, lax.axis_size("tp"))]


def shards_dense(
    block_input,
    segment_ids,
    expert_ids,
    expert_gates,
    attn_norm_gain,
    query_weight,
    key_weight,
    value_projection,
    query_bias,
    key_head_bias,
    value_head_bias,
    sink_head_logits,
    output_weight,
    output_bias,
    ffn_norm_gain,
    gate_weight,
    up_weight,
    gate_bias,
    up_bias,
    down_weight,
    down_bias,
    cotangent,
):
    ep_count = lax.axis_size("ep")
    tp_count = lax.axis_size("tp")
    ep_index = lax.axis_index("ep")
    tp_index = lax.axis_index("tp")
    token_count, width = block_input.shape
    block = token_count // tp_count
    quarter = width // tp_count
    slice_width = width // ep_count
    local_heads = query_weight.shape[1] // HEAD_SIZE
    local_groups = key_weight.shape[1] // HEAD_SIZE
    query_columns = query_weight.shape[1]
    key_columns = key_weight.shape[1]
    query_group_width = QUERY_HEADS // KEY_VALUE_HEADS
    scale_factor = HEAD_SIZE ** (-0.5)

    def own_order(rows):
        return jnp.concatenate(
            [
                lax.dynamic_slice_in_dim(rows, (tp_index ^ r) * block, block, 0)
                for r in range(tp_count)
            ],
            axis=0,
        )

    token_rows = own_order(block_input)
    segments = own_order(segment_ids)
    cotangent_rows = own_order(cotangent)
    ids = own_order(expert_ids)
    gates = own_order(expert_gates)
    places = lax.iota(jnp.int32, token_count)
    places = ((places // block) ^ tp_index) * block + places % block

    chosen = ids[None, :, :] == jnp.arange(ep_count, dtype=jnp.int32)[:, None, None]
    gate_table = jnp.sum(jnp.where(chosen, gates[None], 0.0), axis=2)
    small = [
        attn_norm_gain,
        ffn_norm_gain,
        output_bias,
        query_bias.reshape(-1),
        key_head_bias.reshape(-1),
        value_head_bias.reshape(-1),
    ]
    small = jnp.concatenate([v.astype(jnp.float32) for v in small])
    small_size = small.shape[0]
    pad = -small_size % 128
    small = jnp.concatenate([small, jnp.zeros((pad,), jnp.float32), gate_table.reshape(-1)])[None]
    for mask in (CORE, ACROSS_X, ACROSS_Y):
        small = jnp.concatenate([small, hop(small, mask)], axis=0)
    ordered = jnp.concatenate(
        [lax.dynamic_slice_in_dim(small, ep_index ^ s, 1, 0) for s in range(ep_count)], axis=0
    )
    attn_scale = ordered[:, :slice_width].reshape(width)
    ffn_scale = ordered[:, slice_width : 2 * slice_width].reshape(width)
    out_shift = ordered[:, 2 * slice_width : 3 * slice_width].reshape(width)

    def bias_of(start, heads):
        share = HEAD_SIZE // ep_count
        rows = ordered[:, start : start + heads * share].reshape(ep_count, heads, share)
        return rows.transpose(1, 0, 2).reshape(heads * HEAD_SIZE)

    at = 3 * slice_width
    share = HEAD_SIZE // ep_count
    qkv_shift = jnp.concatenate(
        [
            bias_of(at, local_heads),
            bias_of(at + local_heads * share, local_groups),
            bias_of(at + (local_heads + local_groups) * share, local_groups),
        ]
    )
    route_table = small[:, small_size + pad :].reshape(ep_count, ep_count, token_count)
    route_gate = lax.dynamic_index_in_dim(route_table, ep_index, 1, keepdims=False)
    route_gate = route_gate.reshape(ep_count * token_count, 1)

    qkv_own = jnp.concatenate([query_weight, key_weight, value_projection], axis=1)
    qkv_pieces = gather_plane(qkv_own)
    qkv_matrix = natural_rows(qkv_pieces, ep_index)
    out_own = after(output_weight.T, qkv_pieces[6][0], qkv_pieces[6][1])
    out_pieces = gather_plane(out_own)
    out_matrix = natural_rows(out_pieces, ep_index)
    cotangent_own = after(cotangent_rows, out_pieces[6][0], out_pieces[6][1])
    cotangent_pieces = gather_plane(cotangent_own)

    sink_logit_grid = sink_head_logits.astype(jnp.float32).reshape(local_groups, query_group_width)[
        :, :, None
    ]
    inputs = token_rows.astype(jnp.float32)
    attn_normed, attn_inverse = rms_stats(inputs)
    attn_in = (attn_normed * attn_scale).astype(jnp.bfloat16)
    qkv_heads = jnp.dot(attn_in, qkv_matrix, preferred_element_type=jnp.float32) + qkv_shift
    query_heads = qkv_heads[:, :query_columns]
    key_heads = qkv_heads[:, query_columns : query_columns + key_columns]
    value_heads = qkv_heads[:, query_columns + key_columns :]

    allowed = (segments[:, None] == segments[None, :]) & (places[None, :] <= places[:, None])
    position = jnp.sum(allowed.astype(jnp.float32), axis=1) - 1.0
    frequency = THETA ** (-2.0 * jnp.arange(HEAD_SIZE // 2, dtype=jnp.float32) / HEAD_SIZE)
    angles = position[:, None] * frequency[None, :]
    cosine_table, sine_table = jnp.cos(angles), jnp.sin(angles)

    rotated_query = rotate(
        query_heads.reshape(token_count, local_heads, HEAD_SIZE), cosine_table, sine_table
    ).astype(jnp.bfloat16)
    grouped_heads = rotated_query.reshape(token_count, local_groups, query_group_width, HEAD_SIZE)
    keys_rot = rotate(
        key_heads.reshape(token_count, local_groups, HEAD_SIZE), cosine_table, sine_table
    ).astype(jnp.bfloat16)
    value_cast = value_heads.reshape(token_count, local_groups, HEAD_SIZE).astype(jnp.bfloat16)
    scores = attention_scores(grouped_heads, keys_rot, allowed)
    top_score = jnp.maximum(jnp.max(scores, axis=3), sink_logit_grid)
    total = jnp.sum(jnp.exp(scores - top_score[..., None]), axis=3) + jnp.exp(
        sink_logit_grid - top_score
    )
    log_total = top_score + jnp.log(total)
    probability = jnp.exp(scores - log_total[..., None]).astype(jnp.bfloat16)
    attended_rows = jnp.einsum(
        "ghqk,kga->qgha", probability, value_cast, preferred_element_type=jnp.float32
    )
    attended_rows = attended_rows.reshape(token_count, local_heads * HEAD_SIZE).astype(jnp.bfloat16)
    head_part = lax.dot_general(
        attended_rows, out_matrix, (((1,), (1,)), ((), ())), preferred_element_type=jnp.float32
    )
    residual = inputs[:block] + (sum_tp_blocks(head_part, block) + out_shift)
    ffn_normed, ffn_inverse = rms_stats(residual)
    ffn_own = (ffn_normed * ffn_scale).astype(jnp.bfloat16)
    ffn_rows = jnp.concatenate(gather_tp_blocks(ffn_own), axis=0)
    ffn_pieces = gather_plane(ffn_rows)

    gate_matrix = gate_weight[0]
    up_matrix = up_weight[0]
    down_matrix = down_weight[0]
    route_grads = jnp.concatenate([part for group in cotangent_pieces for part in group], axis=0)
    route_grads = (route_gate * route_grads.astype(jnp.float32)).astype(jnp.bfloat16)
    hidden_grad = lax.dot_general(
        route_grads, down_matrix, (((1,), (1,)), ((), ())), preferred_element_type=jnp.float32
    )
    blocked_sums = jnp.sum(
        route_grads.astype(jnp.float32).reshape(ep_count, tp_count, block, width), axis=(0, 2)
    )
    down_bias_grad = (blocked_sums[0] + blocked_sums[1]) + (blocked_sums[2] + blocked_sums[3])

    spans = ((0, 2), (2, 6), (6, 8))
    kept = []
    for low, high in spans:
        rows = jnp.concatenate([p for group in ffn_pieces[low:high] for p in group], axis=0)
        row_grad = hidden_grad[low * token_count : high * token_count]
        gate_pre = jnp.dot(rows, gate_matrix, preferred_element_type=jnp.float32) + gate_bias[
            0
        ].astype(jnp.float32)
        up_pre = jnp.dot(rows, up_matrix, preferred_element_type=jnp.float32) + up_bias[0].astype(
            jnp.float32
        )
        gate_clip = jnp.minimum(gate_pre, LIMIT)
        up_clip = jnp.clip(up_pre, -LIMIT, LIMIT)
        sigmoid_gate = jax.nn.sigmoid(ALPHA * gate_clip)
        glu_part = gate_clip * sigmoid_gate
        hidden_cast = ((up_clip + 1.0) * glu_part).astype(jnp.bfloat16)
        up_grad = jnp.where((up_pre > -LIMIT) & (up_pre < LIMIT), row_grad * glu_part, 0.0)
        gate_grad = jnp.where(
            gate_pre < LIMIT,
            row_grad
            * (up_clip + 1.0)
            * (sigmoid_gate + ALPHA * gate_clip * sigmoid_gate * (1.0 - sigmoid_gate)),
            0.0,
        )
        kept.append(
            (
                rows,
                hidden_cast,
                gate_grad.astype(jnp.bfloat16),
                up_grad.astype(jnp.bfloat16),
                jnp.sum(gate_grad, axis=0),
                jnp.sum(up_grad, axis=0),
            )
        )
    gate_bias_grad = (kept[0][4] + kept[1][4] + kept[2][4])[None]
    up_bias_grad = (kept[0][5] + kept[1][5] + kept[2][5])[None]

    def rows_of(which, relative):
        for span, entry in zip(spans, kept):
            if span[0] <= relative < span[1]:
                start = (relative - span[0]) * token_count
                return entry[which][start : start + token_count]

    def input_part(relative):
        return lax.dot_general(
            rows_of(2, relative),
            gate_matrix,
            (((1,), (1,)), ((), ())),
            preferred_element_type=jnp.float32,
        ) + lax.dot_general(
            rows_of(3, relative),
            up_matrix,
            (((1,), (1,)), ((), ())),
            preferred_element_type=jnp.float32,
        )

    input_sum = scatter_plane(input_part)

    down_shift = jnp.where(tp_index == 0, down_bias[0].astype(jnp.float32), 0.0)

    def output_part(relative):
        rows = rows_of(1, relative)
        if relative == 7:
            rows = after(rows, input_sum)
        weight = route_gate[relative * token_count : (relative + 1) * token_count]
        return weight * (
            jnp.dot(rows, down_matrix, preferred_element_type=jnp.float32) + down_shift
        )

    ffn_in_grad = sum_tp_blocks(input_sum, block)
    feedforward_gain_grad = jnp.sum(ffn_in_grad * ffn_normed, axis=0)
    grad_out = cotangent_rows[:block].astype(jnp.float32)
    residual_grad = grad_out + norm_back(ffn_in_grad * ffn_scale, ffn_normed, ffn_inverse)
    output_offset_grad = jnp.sum(residual_grad, axis=0)
    residual_cast = jnp.concatenate(
        gather_tp_blocks(residual_grad.astype(jnp.bfloat16)), axis=0
    )

    output_sum = scatter_plane(output_part)
    moe_rows = sum_tp_blocks(output_sum, block)
    result_rows = (residual + moe_rows).astype(jnp.bfloat16)
    result_parts = result_rows.reshape(block, tp_count, quarter).transpose(1, 0, 2)
    held = []
    for relative in range(tp_count):
        part = lax.dynamic_index_in_dim(result_parts, tp_index ^ relative, 0, keepdims=False)
        held.append(hop_tp(part, relative) if relative else part)
    held = jnp.stack(held)
    block_result = jnp.concatenate(
        [lax.dynamic_index_in_dim(held, tp_index ^ q, 0, keepdims=False) for q in range(tp_count)],
        axis=0,
    )

    all_rows = jnp.concatenate([entry[0] for entry in kept], axis=0)
    all_gate = jnp.concatenate([entry[2] for entry in kept], axis=0)
    all_up = jnp.concatenate([entry[3] for entry in kept], axis=0)
    all_hidden = jnp.concatenate([entry[1] for entry in kept], axis=0)

    def over_rows(left, right):
        return lax.dot_general(
            left, right, (((0,), (0,)), ((), ())), preferred_element_type=jnp.float32
        )

    gate_weight_grad = over_rows(all_rows, all_gate)[None]
    up_weight_grad = over_rows(all_rows, all_up)[None]
    down_weight_grad = over_rows(all_hidden, route_grads)[None]

    attended_grad = jnp.dot(
        residual_cast, out_matrix, preferred_element_type=jnp.float32
    ).astype(jnp.bfloat16)
    out_matrix_grad = over_rows(residual_cast, attended_rows).astype(jnp.bfloat16)
    out_matrix_grad = out_matrix_grad.reshape(ep_count, slice_width, query_columns)
    output_projection_grad = scatter_plane(
        lambda r: lax.dynamic_index_in_dim(out_matrix_grad, ep_index ^ r, 0, keepdims=False)
    ).T

    head_gradients = attended_grad.reshape(token_count, local_groups, query_group_width, HEAD_SIZE)
    softmax_delta = jnp.einsum(
        "nxiz,nxiz->xin",
        head_gradients,
        attended_rows.reshape(token_count, local_groups, query_group_width, HEAD_SIZE),
        preferred_element_type=jnp.float32,
    )
    scores = attention_scores(grouped_heads, keys_rot, allowed)
    probability = jnp.exp(scores - log_total[..., None])
    prob_cast = probability.astype(jnp.bfloat16)
    value_gradient = jnp.einsum(
        "ghqk,qgha->kga", prob_cast, head_gradients, preferred_element_type=jnp.float32
    )
    prob_grad = jnp.einsum(
        "qgha,kga->ghqk", head_gradients, value_cast, preferred_element_type=jnp.float32
    )
    score_grad = (probability * (prob_grad - softmax_delta[..., None])).astype(jnp.bfloat16)
    query_rot_grad = (
        jnp.einsum("ghqk,kga->qgha", score_grad, keys_rot, preferred_element_type=jnp.float32)
        * scale_factor
    )
    keys_rot_grad = (
        jnp.einsum("ghqk,qgha->kga", score_grad, grouped_heads, preferred_element_type=jnp.float32)
        * scale_factor
    )
    sink_weight_term = -jnp.sum(
        jnp.exp(sink_logit_grid - log_total) * softmax_delta, axis=2
    ).reshape(local_heads)
    query_gradient = unrotate(
        query_rot_grad.reshape(token_count, local_heads, HEAD_SIZE), cosine_table, sine_table
    ).reshape(token_count, query_columns)
    key_gradient = unrotate(keys_rot_grad, cosine_table, sine_table).reshape(
        token_count, key_columns
    )
    value_gradient = value_gradient.reshape(token_count, key_columns)
    qkv_gradient = jnp.concatenate([query_gradient, key_gradient, value_gradient], axis=1)
    qkv_cast = qkv_gradient.astype(jnp.bfloat16)
    attn_in_part = lax.dot_general(
        qkv_cast, qkv_matrix, (((1,), (1,)), ((), ())), preferred_element_type=jnp.float32
    )
    attn_in_grad = sum_tp_blocks(attn_in_part, block)
    qkv_matrix_grad = over_rows(attn_in, qkv_cast).astype(jnp.bfloat16)
    qkv_matrix_grad = qkv_matrix_grad.reshape(ep_count, slice_width, qkv_cast.shape[1])
    qkv_weight_grad = scatter_plane(
        lambda r: lax.dynamic_index_in_dim(qkv_matrix_grad, ep_index ^ r, 0, keepdims=False)
    )
    query_projection_grad = qkv_weight_grad[:, :query_columns]
    key_projection_grad = qkv_weight_grad[:, query_columns : query_columns + key_columns]
    value_projection_grad = qkv_weight_grad[:, query_columns + key_columns :]

    attn_normed_own = attn_normed[:block]
    attn_gain_grad = jnp.sum(attn_in_grad * attn_normed_own, axis=0)
    input_grad_own = (
        residual_grad
        + norm_back(attn_in_grad * attn_scale, attn_normed_own, attn_inverse[:block])
    ).astype(jnp.bfloat16)
    input_grad_parts = jnp.stack(gather_tp_blocks(input_grad_own))
    block_input_grad = jnp.concatenate(
        [
            lax.dynamic_index_in_dim(input_grad_parts, tp_index ^ q, 0, keepdims=False)
            for q in range(tp_count)
        ],
        axis=0,
    )

    def sum_all(value, axes):
        if "tp" in axes:
            for mask in (1, 2):
                value = value + hop_tp(value, mask)
        if "ep" in axes:
            for mask in (CORE, ACROSS_X, ACROSS_Y):
                value = value + hop(value, mask)
        return value

    early = sum_all(jnp.stack([feedforward_gain_grad, output_offset_grad]), ("tp", "ep"))
    early = lax.dynamic_index_in_dim(
        early.reshape(2, ep_count, slice_width), ep_index, 1, keepdims=False
    )
    sums = jnp.concatenate([jnp.sum(qkv_gradient, axis=0), sink_weight_term])
    sums = sum_all(sums, ("ep",))
    head_sums = sums[: qkv_cast.shape[1]].reshape(-1, ep_count, share)
    head_sums = lax.dynamic_index_in_dim(head_sums, ep_index, 1, keepdims=False)
    late = sum_all(attn_gain_grad, ("tp", "ep"))
    late = lax.dynamic_index_in_dim(
        late.reshape(ep_count, slice_width), ep_index, 0, keepdims=False
    )
    return (
        block_result,
        block_input_grad,
        late,
        query_projection_grad,
        key_projection_grad,
        value_projection_grad,
        head_sums[:local_heads],
        head_sums[local_heads : local_heads + local_groups],
        head_sums[local_heads + local_groups :],
        sums[qkv_cast.shape[1] :],
        output_projection_grad,
        early[1],
        early[0],
        gate_weight_grad,
        up_weight_grad,
        gate_bias_grad,
        up_bias_grad,
        down_weight_grad,
        down_bias_grad[None],
    )


def solution(mesh):
    in_specs = (
        P("ep", None),
        P("ep"),
        P("ep", None),
        P("ep", None),
        P("ep"),
        P("ep", "tp"),
        P("ep", "tp"),
        P("ep", "tp"),
        P("tp", "ep"),
        P("tp", "ep"),
        P("tp", "ep"),
        P("tp"),
        P("tp", "ep"),
        P("ep"),
        P("ep"),
        P("ep", None, "tp"),
        P("ep", None, "tp"),
        P("ep", "tp"),
        P("ep", "tp"),
        P("ep", "tp", None),
        P("ep", None),
        P("ep", None),
    )
    out_specs = (
        P("ep", "tp"),
        P("ep", None),
        P("ep"),
        P("ep", "tp"),
        P("ep", "tp"),
        P("ep", "tp"),
        P("tp", "ep"),
        P("tp", "ep"),
        P("tp", "ep"),
        P("tp"),
        P("tp", "ep"),
        P("ep"),
        P("ep"),
        P("ep", None, "tp"),
        P("ep", None, "tp"),
        P("ep", "tp"),
        P("ep", "tp"),
        P("ep", "tp", None),
        P("ep", None),
    )
    body = shards_dense if (mesh.shape["ep"], mesh.shape["tp"]) == (8, 4) else shards_routed
    return jax.shard_map(body, mesh=mesh, in_specs=in_specs, out_specs=out_specs, check_vma=False)
```
